32 devices in a mesh: ens: 2 (over y), mem: 4 (over x, core), lon: 4 (over z).
Axes of the slice: x: 2, y: 2, z: 4, core: 2. Of those that a mesh axis runs over, the one named last changes fastest.
Arguments:
- initial_state: float32 [8, 4, 4, 256, 128], P(('ens', 'mem'), None, None, 'lon'), parts along dimension 0, may hold values from -1.25 to 1.25
- ancestor: int32 [8], P(('ens', 'mem')), parts along dimension 0, may hold values from 0 to 3
- selector: int32 [8], P(('ens', 'mem')), parts along dimension 0, may hold values from 0 to 3
- perturbations: float32 [8, 4, 4, 256, 128], P('ens', None, None, 'lon'), parts along dimension 0, may hold values from -0.5 to 0.5
- diffusivity: float32 [4, 256, 128], P(None, 'lon'), may hold values from 0.05 to 0.3
- region_weight: float32 [256, 128], P('lon'), may hold values from 0.3 to 27, as said below
Outputs:
- final_state: float32 [8, 4, 4, 256, 128], P(('ens', 'mem'), None, None, 'lon'), parts along dimension 0
- actions: float32 [8, 2], P(('ens', 'mem')), parts along dimension 0
The draws below stay inside these ranges and needn't reach their ends.
There are 2 independent parts, one for each index of `ens`. The reference program is written for one: setup_inputs(seed, part) draws one part's arguments, and reference() takes and returns one part's arrays. A program takes and returns all parts, laid end to end along the dimension named above; an argument that names none is the same for every part. Nothing has to cross between parts.
Inputs may be any that keep to these rules, and one draw needn't show every extreme that they name: `region_weight`: Positive.
All inputs are finite; a program needn't handle non-finite values.
Results may differ from the reference program's by a relative error of at most 0.0001.
Values sent between devices are 32-bit elements; how exact they have to be, the bound alone decides.
A program may use at most 64 MiB of HBM per device.

```python
import math
import jax
import jax.numpy as jnp
import numpy as np

FIELDS = 4
LAT = 128
LEV = 4
NPERT = 4
STEPS = 3
LON = 256
MEMBERS = 4


def draw_region_weight(key, part):
    base = jax.random.uniform(key, (LON, LAT), jnp.float32, jnp.log(0.3), jnp.log(3.0))
    ramp = jnp.log(3.0) * jnp.arange(LON, dtype=jnp.float32)[:, None] / LON
    return jnp.exp(base + ramp)


def with_ends(entries, own_key, low, top_value):
    longest = entries.shape.index(max(entries.shape))
    spots = []
    for shift in (0, 1):
        where = [jax.random.randint(jax.random.fold_in(own_key, axis), (), 0, length) for axis, length in enumerate(entries.shape)]
        where[longest] = (where[longest] + shift) % entries.shape[longest]
        spots.append(tuple(where))
    return entries.at[spots[0]].set(low).at[spots[1]].set(top_value)


def block_scale(key, dims, pieces, low, high):
    factor_of = 1.0
    for dim, blocks in pieces:
        steps = jax.random.uniform(jax.random.fold_in(jax.random.fold_in(key, 6), dim), (blocks,), jnp.float32, low / len(pieces), high / len(pieces))
        factor_of = factor_of * jnp.repeat(jnp.exp(steps), dims[dim] // blocks).reshape((-1,) + (1,) * (len(dims) - 1 - dim))
    return factor_of


def rank_table(count, slope):
    weights = [(1 << 20) // math.isqrt(standing ** slope) + 1 for standing in range(1, count + 1)]
    width = 1 + sum(weights) // (1 << 30)
    return np.cumsum(np.array([max(1, weight // width) for weight in weights]))


def skewed_ids(stream_key, extent, count, slope):
    table = rank_table(count, slope)
    ticket = jax.random.randint(jax.random.fold_in(stream_key, 1), extent, 0, int(table[count - 1]))
    rank = jnp.searchsorted(jnp.asarray(table, jnp.int32), ticket, side="right")
    return jax.random.permutation(jax.random.fold_in(stream_key, 2), count)[rank].astype(jnp.int32)


def normal_values(rng, shape, width, limit, shards=(), held_as=jnp.bfloat16):
    array = jax.random.normal(rng, shape, jnp.float32) * width
    if len(shards) > 0:
        array = block_scale(rng, shape, shards, -0.22, 0.18) * array
    return jnp.clip(array, min=-limit, max=limit).astype(held_as)


def setup_inputs(seed: int = 0, part: int = 0) -> dict:
    key_list = jax.random.split(jax.random.key(seed), 7)
    own_keys = jax.random.split(jax.random.fold_in(key_list[6], part), 7)
    return {
        "initial_state": normal_values(own_keys[0], (MEMBERS, FIELDS, LEV, LON, LAT), 0.5, 1.25, ((0, 4), (3, 4)), jnp.float32),
        "ancestor": with_ends(skewed_ids(own_keys[1], (MEMBERS,), MEMBERS, 2), jax.random.fold_in(own_keys[1], 3), 0, MEMBERS - 1).astype(jnp.int32),
        "selector": with_ends(jax.random.randint(own_keys[2], (MEMBERS,), 0, NPERT), jax.random.fold_in(own_keys[2], 1), 0, NPERT - 1).astype(jnp.int32),
        "perturbations": normal_values(own_keys[3], (NPERT, FIELDS, LEV, LON, LAT), 0.2, 0.5, ((3, 4),), jnp.float32),
        "diffusivity": jnp.clip(0.05 + 0.25 * jax.random.uniform(key_list[4], (LEV, LON, LAT), jnp.float32) ** block_scale(key_list[4], (LEV, LON, LAT), ((1, 4),), -0.2, 0.2), 0.05, 0.3),
        "region_weight": draw_region_weight(jax.random.fold_in(key_list[6], 71), part),
    }


TIME_STEP = 0.2


def shifted_lat(tracer_field, upward_flux):
    if upward_flux:
        return jnp.concatenate([tracer_field[..., 1:], tracer_field[..., -1:]], axis=-1)
    return jnp.concatenate([tracer_field[..., :1], tracer_field[..., :-1]], axis=-1)


def cycle_pad(tracer_field):
    return jnp.concatenate([tracer_field[..., -1:, :], tracer_field, tracer_field[..., :1, :]], axis=-2)


def advance(padded, kappa_pad):
    centre = padded[..., 1:-1, :]
    west_cell = padded[..., :-2, :]
    east_cell = padded[..., 2:, :]
    south_cell = shifted_lat(centre, False)
    north_cell = shifted_lat(centre, True)
    kappa_mid = kappa_pad[..., 1:-1, :]
    kappa_west = 0.5 * (kappa_mid + kappa_pad[..., :-2, :])
    kappa_east = 0.5 * (kappa_mid + kappa_pad[..., 2:, :])
    kappa_south = 0.5 * (kappa_mid + shifted_lat(kappa_mid, False))
    kappa_north = 0.5 * (kappa_mid + shifted_lat(kappa_mid, True))
    zonal_wind = centre[:, 0:1]
    merid_wind = centre[:, 1:2]
    transport = (jnp.maximum(zonal_wind, 0.0) * (centre - west_cell)
                 + jnp.minimum(zonal_wind, 0.0) * (east_cell - centre)
                 + jnp.maximum(merid_wind, 0.0) * (centre - south_cell)
                 + jnp.minimum(merid_wind, 0.0) * (north_cell - centre))
    mixing = (kappa_east * (east_cell - centre) - kappa_west * (centre - west_cell)
              + kappa_north * (north_cell - centre) - kappa_south * (centre - south_cell))
    return centre + TIME_STEP * (mixing - transport)


def measure(tracer_field, clone_weight):
    thermal_field = tracer_field[:, 2]
    return jnp.sum(clone_weight * thermal_field * thermal_field, axis=(1, 2, 3))


def reference(initial_state, ancestor, selector, perturbations, diffusivity, region_weight):
    kappa_pad = cycle_pad(diffusivity)
    cell_count = LEV * LON * LAT

    def integrate_block(present_state):
        running = jnp.zeros((present_state.shape[0],), jnp.float32)
        for section in range(STEPS):
            present_state = advance(cycle_pad(present_state), kappa_pad)
            running = running + measure(present_state, region_weight) / cell_count
        return present_state, running

    middle, first_action = integrate_block(initial_state)
    cloned = jnp.take(middle, ancestor, axis=0) + jnp.take(perturbations, selector, axis=0)
    final_state, second_action = integrate_block(cloned)
    return final_state, jnp.stack([first_action, second_action], axis=1)
```

```python
import functools

import jax
import jax.numpy as jnp
from jax import lax
from jax.experimental import pallas as pl
from jax.experimental.pallas import tpu as pltpu
from jax.sharding import PartitionSpec as P

STEPS = 3
TIME_STEP = 0.2
EDGE = 8
MESH_ID = pl.DeviceIdType.MESH


def kernel(
    n, ring, anc_ref, sel_ref, init_ref, pert_ref, kap_ref, weight_ref, out_ref, act_ref,
    full, state, own, pert, pert_edge, pert_halo, edge, kap, face, coef, weight, part,
    x_send, x_recv, p_send, p_recv, z_send, z_recv, s_send, s_recv, local_sem,
):
    _, fields, levels, width, lat = init_ref.shape
    rows = width + 2 * EDGE
    dyn = fields - 1
    groups = n // 2
    mem = lax.axis_index("mem")
    lon = lax.axis_index("lon")
    twin = mem + 1 - 2 * lax.rem(mem, 2)
    east, west = lax.rem(lon + 1, ring), lax.rem(lon + ring - 1, ring)
    top = width - EDGE

    local = [
        pltpu.make_async_copy(init_ref.at[0], full.at[mem], local_sem.at[0]),
        pltpu.make_async_copy(
            init_ref.at[0, pl.ds(0, dyn)], own.at[:, :, pl.ds(EDGE, width)], local_sem.at[1]
        ),
        pltpu.make_async_copy(kap_ref, kap.at[:, pl.ds(EDGE, width)], local_sem.at[2]),
        pltpu.make_async_copy(weight_ref, weight, local_sem.at[3]),
        pltpu.make_async_copy(pert_ref, pert, local_sem.at[4]),
    ]
    for copy in local:
        copy.start()

    barrier = pltpu.get_barrier_semaphore()
    peers = 0
    for k in range(1, groups):
        pl.semaphore_signal(
            barrier, inc=1, device_id={"mem": lax.rem(mem + 2 * k, n)}, device_id_type=MESH_ID
        )
        peers += 1
    pl.semaphore_signal(barrier, inc=1, device_id={"mem": twin}, device_id_type=MESH_ID)
    peers += 1
    for d in range(1, ring):
        pl.semaphore_signal(
            barrier, inc=1, device_id={"lon": lax.rem(lon + d, ring)}, device_id_type=MESH_ID
        )
        peers += 1
    pl.semaphore_wait(barrier, peers)

    def view(block, kind, level):
        if kind == "lo":
            return block.at[:, :, pl.ds(0, EDGE)]
        if kind == "hi":
            return block.at[:, :, pl.ds(top, EDGE)]
        if kind == "dyn":
            return block.at[pl.ds(0, dyn), level, pl.ds(EDGE, width - 2 * EDGE)]
        return block.at[dyn, level, pl.ds(EDGE, width - 2 * EDGE)]

    def sem_of(kind, level):
        return {"lo": 0, "hi": 1, "dyn": 2 + level, "hum": 2 + levels + level}[kind]

    def across(k, kind, level):
        slot = sem_of(kind, level)
        return pltpu.make_async_remote_copy(
            src_ref=view(init_ref.at[0], kind, level),
            dst_ref=view(full.at[mem], kind, level),
            send_sem=x_send.at[k - 1, slot],
            recv_sem=x_recv.at[k - 1, slot],
            device_id={"mem": lax.rem(mem + 2 * k, n)},
            device_id_type=MESH_ID,
        )

    def to_twin(k, kind, level):
        slot = sem_of(kind, level)
        member = lax.rem(mem + n - 2 * k, n)
        source = init_ref.at[0] if k == 0 else full.at[member]
        return pltpu.make_async_remote_copy(
            src_ref=view(source, kind, level),
            dst_ref=view(full.at[member], kind, level),
            send_sem=p_send.at[k, slot],
            recv_sem=p_recv.at[k, slot],
            device_id={"mem": twin},
            device_id_type=MESH_ID,
        )

    def lon_copy(source, target, slot, side):
        return pltpu.make_async_remote_copy(
            src_ref=source,
            dst_ref=target,
            send_sem=z_send.at[slot, side],
            recv_sem=z_recv.at[slot, side],
            device_id={"lon": east if side else west},
            device_id_type=MESH_ID,
        )

    low, high = pl.ds(0, EDGE), pl.ds(EDGE + width, EDGE)
    first, last = pl.ds(0, EDGE), pl.ds(top, EDGE)
    pieces = [("lo", 0), ("hi", 0)]
    pieces += [("dyn", level) for level in range(levels)]
    pieces += [("hum", level) for level in range(levels)]
    for kind, level in pieces:
        for k in range(1, groups):
            across(k, kind, level).start()
    own_halo = [
        lon_copy(init_ref.at[0, pl.ds(0, dyn), :, first], own.at[:, :, high], 0, 0),
        lon_copy(init_ref.at[0, pl.ds(0, dyn), :, last], own.at[:, :, low], 0, 1),
    ]
    kap_halo = [
        lon_copy(kap_ref.at[:, first], kap.at[:, high], 1, 0),
        lon_copy(kap_ref.at[:, last], kap.at[:, low], 1, 1),
    ]
    for copy in kap_halo + own_halo:
        copy.start()
    for kind, level in pieces:
        to_twin(0, kind, level).start()

    local[4].wait()
    chosen = sel_ref[0]
    for f in range(fields):
        for level in range(levels):
            pert_edge[0, f, level] = pert[chosen, f, level, 0:EDGE, :]
            pert_edge[1, f, level] = pert[chosen, f, level, top:width, :]
    pert_copy = [
        lon_copy(pert_edge.at[0], pert_halo.at[1], 2, 0),
        lon_copy(pert_edge.at[1], pert_halo.at[0], 2, 1),
    ]
    for copy in pert_copy:
        copy.start()

    for copy in local[:4]:
        copy.wait()
    for copy in kap_halo:
        copy.wait()

    lane = lax.broadcasted_iota(jnp.int32, (rows, lat), 1)
    not_north = jnp.where(lane == lat - 1, 0.0, 1.0)
    not_south = jnp.where(lane == 0, 0.0, 1.0)

    def from_west(q):
        return pltpu.roll(q, 1, 0)

    def from_east(q):
        return pltpu.roll(q, rows - 1, 0)

    def from_south(q):
        return pltpu.roll(q, 1, 1)

    def from_north(q):
        return pltpu.roll(q, lat - 1, 1)

    def faces(level, _):
        k = kap[level]
        to_east = (0.5 * TIME_STEP) * (k + from_east(k))
        to_north = (0.5 * TIME_STEP) * (k + from_north(k)) * not_north
        face[0, level] = to_east
        face[1, level] = from_west(to_east)
        face[2, level] = to_north
        face[3, level] = from_south(to_north)
        return 0

    lax.fori_loop(0, levels, faces, 0)

    def coefficients(u, v, level):
        u = TIME_STEP * u
        v = TIME_STEP * v
        to_e = face[0, level] - jnp.minimum(u, 0.0)
        to_w = face[1, level] + jnp.maximum(u, 0.0)
        to_n = face[2, level] - jnp.minimum(v, 0.0) * not_north
        to_s = face[3, level] + jnp.maximum(v, 0.0) * not_south
        here = 1.0 - ((to_e + to_w) + (to_n + to_s))
        return to_e, to_w, to_n, to_s, here

    def moved(q, c):
        to_e, to_w, to_n, to_s, here = c
        return (
            here * q
            + (to_e * from_east(q) + to_w * from_west(q))
            + (to_n * from_north(q) + to_s * from_south(q))
        )

    def observed(t):
        inner = t[EDGE : EDGE + width, :]
        terms = weight[...] * inner * inner
        return jnp.sum(terms.reshape(width // 8, 8, lat), axis=0)

    for copy in own_halo:
        copy.wait()

    def own_level(level, total):
        u, v, t = own[0, level], own[1, level], own[2, level]
        for step in range(STEPS):
            c = coefficients(u, v, level)
            t_next = moved(t, c)
            if step < STEPS - 1:
                u, v = moved(u, c), moved(v, c)
            t = t_next
            total = total + observed(t)
        return total

    part[0, lon] = lax.fori_loop(0, levels, own_level, jnp.zeros((8, lat), jnp.float32))

    def share(which):
        return [
            pltpu.make_async_remote_copy(
                src_ref=part.at[which, lon],
                dst_ref=part.at[which, lon],
                send_sem=s_send.at[which, d - 1],
                recv_sem=s_recv.at[which, d - 1],
                device_id={"lon": lax.rem(lon + d, ring)},
                device_id_type=MESH_ID,
            )
            for d in range(1, ring)
        ]

    def arrive(kind, level):
        for k in range(1, groups):
            across(k, kind, level).wait_recv()
            to_twin(k, kind, level).start()

    def settled(kind, level):
        for k in range(groups):
            to_twin(k, kind, level).wait_recv()

    arrive("lo", 0)
    arrive("hi", 0)
    first_share = share(0)
    for copy in first_share:
        copy.start()
    settled("lo", 0)
    settled("hi", 0)
    ancestor = anc_ref[0]

    def pick(load):
        value = load(0)
        for j in range(1, n):
            value = jnp.where(ancestor == j, load(j), value)
        return value

    for f in range(fields):
        for level in range(levels):
            lower = pick(lambda j: full[j, f, level, 0:EDGE, :])
            upper = pick(lambda j: full[j, f, level, top:width, :])
            edge[0, f, level] = lower
            edge[1, f, level] = upper
            state[f, level, EDGE : 2 * EDGE, :] = lower
            state[f, level, width : width + EDGE, :] = upper
    edge_copy = [
        lon_copy(edge.at[0], state.at[:, :, high], 3, 0),
        lon_copy(edge.at[1], state.at[:, :, low], 3, 1),
    ]
    for copy in edge_copy:
        copy.start()
    arrive("dyn", 0)
    for copy in pert_copy + edge_copy:
        copy.wait()

    def fill(f, level):
        state[f, level, 2 * EDGE : width, :] = pick(
            lambda j: full[j, f, level, EDGE : width - EDGE, :]
        )
        return state[f, level]

    def noise(f, level):
        return jnp.concatenate(
            [pert_halo[0, f, level], pert[chosen, f, level], pert_halo[1, f, level]], axis=0
        )

    def dyn_level(level, total):
        @pl.when(level < levels - 1)
        def _():
            arrive("dyn", level + 1)

        @pl.when(level == levels - 1)
        def _():
            arrive("hum", 0)

        settled("dyn", level)
        u, v, t = fill(0, level), fill(1, level), fill(2, level)
        for step in range(2 * STEPS):
            if step == STEPS:
                u, v, t = u + noise(0, level), v + noise(1, level), t + noise(2, level)
            c = coefficients(u, v, level)
            for i in range(5):
                coef[level, step, i] = c[i]
            u, v, t = moved(u, c), moved(v, c), moved(t, c)
            if step >= STEPS:
                total = total + observed(t)
        inner = slice(EDGE, EDGE + width)
        out_ref[0, 0, level] = u[inner]
        out_ref[0, 1, level] = v[inner]
        out_ref[0, 2, level] = t[inner]
        return total

    part[1, lon] = lax.fori_loop(0, levels, dyn_level, jnp.zeros((8, lat), jnp.float32))
    second_share = share(1)
    for copy in second_share:
        copy.start()

    def hum_level(level, carry):
        @pl.when(level < levels - 1)
        def _():
            arrive("hum", level + 1)

        settled("hum", level)
        q = fill(dyn, level)
        for step in range(2 * STEPS):
            if step == STEPS:
                q = q + noise(dyn, level)
            q = moved(q, [coef[level, step, i] for i in range(5)])
        out_ref[0, dyn, level] = q[EDGE : EDGE + width]
        return carry

    lax.fori_loop(0, levels, hum_level, 0)

    cells = levels * lat * width * ring
    for which, copies in enumerate((first_share, second_share)):
        for copy in copies:
            copy.wait()
        act_ref[0, which] = jnp.sum(jnp.sum(part[which], axis=0)) / cells
    for kind, level in pieces:
        for k in range(1, groups):
            across(k, kind, level).wait_send()
        for k in range(groups):
            to_twin(k, kind, level).wait_send()


def body(initial_state, ancestor, selector, perturbations, diffusivity, region_weight):
    n, ring = lax.axis_size("mem"), lax.axis_size("lon")
    _, fields, levels, width, lat = initial_state.shape
    rows = width + 2 * EDGE
    kinds = 2 + 2 * levels
    f32 = jnp.float32
    any_space = pl.BlockSpec(memory_space=pl.ANY)
    smem = pl.BlockSpec(memory_space=pltpu.SMEM)
    dma = pltpu.SemaphoreType.DMA
    return pl.pallas_call(
        functools.partial(kernel, n, ring),
        out_shape=(
            jax.ShapeDtypeStruct(initial_state.shape, f32),
            jax.ShapeDtypeStruct((1, 2), f32),
        ),
        in_specs=[smem, smem, any_space, any_space, any_space, any_space],
        out_specs=(pl.BlockSpec(memory_space=pltpu.VMEM), smem),
        scratch_shapes=[
            pltpu.VMEM((n, fields, levels, width, lat), f32),
            pltpu.VMEM((fields, levels, rows, lat), f32),
            pltpu.VMEM((fields - 1, levels, rows, lat), f32),
            pltpu.VMEM(perturbations.shape, f32),
            pltpu.VMEM((2, fields, levels, EDGE, lat), f32),
            pltpu.VMEM((2, fields, levels, EDGE, lat), f32),
            pltpu.VMEM((2, fields, levels, EDGE, lat), f32),
            pltpu.VMEM((levels, rows, lat), f32),
            pltpu.VMEM((4, levels, rows, lat), f32),
            pltpu.VMEM((levels, 2 * STEPS, 5, rows, lat), f32),
            pltpu.VMEM((width, lat), f32),
            pltpu.VMEM((2, ring, 8, lat), f32),
            dma((n // 2 - 1, kinds)),
            dma((n // 2 - 1, kinds)),
            dma((n // 2, kinds)),
            dma((n // 2, kinds)),
            dma((4, 2)),
            dma((4, 2)),
            dma((2, ring - 1)),
            dma((2, ring - 1)),
            dma((5,)),
        ],
        compiler_params=pltpu.CompilerParams(
            collective_id=0, has_side_effects=True, vmem_limit_bytes=40 * 1024 * 1024
        ),
    )(ancestor, selector, initial_state, perturbations, diffusivity, region_weight)


def solution(mesh):
    in_specs = (
        P(("ens", "mem"), None, None, "lon", None),
        P(("ens", "mem")),
        P(("ens", "mem")),
        P("ens", None, None, "lon", None),
        P(None, "lon", None),
        P("lon", None),
    )
    out_specs = (P(("ens", "mem"), None, None, "lon", None), P(("ens", "mem"), None))
    return jax.shard_map(body, mesh=mesh, in_specs=in_specs, out_specs=out_specs, check_vma=False)
```

```python
import functools

import jax
import jax.numpy as jnp
from jax import lax
from jax.experimental import pallas as pl
from jax.experimental.pallas import tpu as pltpu
from jax.sharding import PartitionSpec as P

STEPS = 3
TIME_STEP = 0.2
EDGE = 8
VMEM_LIMIT = 66000000
MESH_ID = pl.DeviceIdType.MESH


def kernel(
    n, ring, anc_hbm, sel_hbm, init_ref, pert_ref, kap_ref, weight_ref, out_ref, act_ref,
    full, state, own, pert, pert_edge, pert_halo, edge, kap, face, coef, weight, part,
    x_send, x_recv, p_send, p_recv, z_send, z_recv, s_send, s_recv, local_sem,
    token, anc_ref, sel_ref,
):
    _, fields, levels, width, lat = init_ref.shape
    rows = width + 2 * EDGE
    dyn = fields - 1
    groups = n // 2
    mem = lax.axis_index("mem")
    lon = lax.axis_index("lon")
    twin = mem + 1 - 2 * lax.rem(mem, 2)
    east, west = lax.rem(lon + 1, ring), lax.rem(lon + ring - 1, ring)
    top = width - EDGE

    local = [
        pltpu.make_async_copy(init_ref.at[0], full.at[mem], local_sem.at[0]),
        pltpu.make_async_copy(
            init_ref.at[0, pl.ds(0, dyn)], own.at[:, :, pl.ds(EDGE, width)], local_sem.at[1]
        ),
        pltpu.make_async_copy(kap_ref, kap.at[:, pl.ds(EDGE, width)], local_sem.at[2]),
        pltpu.make_async_copy(weight_ref, weight, local_sem.at[3]),
        pltpu.make_async_copy(pert_ref, pert, local_sem.at[4]),
        pltpu.make_async_copy(anc_hbm, anc_ref, local_sem.at[5]),
        pltpu.make_async_copy(sel_hbm, sel_ref, local_sem.at[6]),
    ]
    for copy in local:
        copy.start()

    barrier = pltpu.get_barrier_semaphore()
    for k in range(1, groups):
        pl.semaphore_signal(
            barrier, inc=1, device_id={"mem": lax.rem(mem + 2 * k, n)}, device_id_type=MESH_ID
        )
    pl.semaphore_signal(barrier, inc=1, device_id={"mem": twin}, device_id_type=MESH_ID)

    def toward(semaphore, up):
        @pl.when(lon < ring - 1 if up else lon > 0)
        def _():
            pl.semaphore_signal(
                semaphore, inc=1, device_id={"lon": east if up else west}, device_id_type=MESH_ID
            )

    toward(barrier, True)
    toward(barrier, False)
    beside = jnp.where(lon > 0, 1, 0) + jnp.where(lon < ring - 1, 1, 0)
    pl.semaphore_wait(barrier, groups + beside)

    def pass_token(up):
        @pl.when(lon > 0 if up else lon < ring - 1)
        def _():
            pl.semaphore_wait(token.at[int(up)], 1)

        toward(token.at[int(up)], up)

    def view(block, kind, level):
        if kind == "lo":
            return block.at[pl.ds(0, dyn), :, pl.ds(0, EDGE)]
        if kind == "hi":
            return block.at[pl.ds(0, dyn), :, pl.ds(top, EDGE)]
        if kind == "hum_lo":
            return block.at[dyn, :, pl.ds(0, EDGE)]
        if kind == "hum_hi":
            return block.at[dyn, :, pl.ds(top, EDGE)]
        if kind == "dyn":
            return block.at[pl.ds(0, dyn), level, pl.ds(EDGE, width - 2 * EDGE)]
        return block.at[dyn, level, pl.ds(EDGE, width - 2 * EDGE)]

    def sem_of(kind, level):
        base = {"lo": 0, "hi": 1, "hum_lo": 2, "hum_hi": 3, "dyn": 4, "hum": 4 + levels}
        return base[kind] + level

    def across(k, kind, level):
        slot = sem_of(kind, level)
        return pltpu.make_async_remote_copy(
            src_ref=view(init_ref.at[0], kind, level),
            dst_ref=view(full.at[mem], kind, level),
            send_sem=x_send.at[k - 1, slot],
            recv_sem=x_recv.at[k - 1, slot],
            device_id={"mem": lax.rem(mem + 2 * k, n)},
            device_id_type=MESH_ID,
        )

    def to_twin(k, kind, level):
        slot = sem_of(kind, level)
        member = lax.rem(mem + n - 2 * k, n)
        source = init_ref.at[0] if k == 0 else full.at[member]
        return pltpu.make_async_remote_copy(
            src_ref=view(source, kind, level),
            dst_ref=view(full.at[member], kind, level),
            send_sem=p_send.at[k, slot],
            recv_sem=p_recv.at[k, slot],
            device_id={"mem": twin},
            device_id_type=MESH_ID,
        )

    def lon_copy(source, target, slot, side):
        return pltpu.make_async_remote_copy(
            src_ref=source,
            dst_ref=target,
            send_sem=z_send.at[slot, side],
            recv_sem=z_recv.at[slot, side],
            device_id={"lon": east if side else west},
            device_id_type=MESH_ID,
        )

    low, high = pl.ds(0, EDGE), pl.ds(EDGE + width, EDGE)
    first, last = pl.ds(0, EDGE), pl.ds(top, EDGE)
    pieces = [("lo", 0), ("hi", 0), ("hum_lo", 0), ("hum_hi", 0)]
    pieces += [("dyn", level) for level in range(levels)]
    pieces += [("hum", level) for level in range(levels)]
    for kind, level in pieces:
        for k in range(1, groups):
            across(k, kind, level).start()
    for kind, level in pieces:
        to_twin(0, kind, level).start()

    @pl.when(2 * lon < ring)
    def _():
        pass_token(True)
        pass_token(False)

    @pl.when(2 * lon >= ring)
    def _():
        pass_token(False)
        pass_token(True)

    own_halo = [
        lon_copy(init_ref.at[0, pl.ds(0, dyn), :, first], own.at[:, :, high], 0, 0),
        lon_copy(init_ref.at[0, pl.ds(0, dyn), :, last], own.at[:, :, low], 0, 1),
    ]
    kap_halo = [
        lon_copy(kap_ref.at[:, first], kap.at[:, high], 1, 0),
        lon_copy(kap_ref.at[:, last], kap.at[:, low], 1, 1),
    ]
    for copy in kap_halo:
        copy.start()

    for copy in local:
        copy.wait()
    chosen = sel_ref[0]
    packed = pert_edge.shape[2]
    for level in range(levels):
        for f in range(fields):
            spot = pl.ds(f * STEPS, STEPS)
            pert_edge[0, level, spot, :] = pert[chosen, f, level, 0:STEPS, :]
            pert_edge[1, level, spot, :] = pert[chosen, f, level, width - STEPS : width, :]
        if packed > fields * STEPS:
            rest = packed - fields * STEPS
            for side in range(2):
                pert_edge[side, level, pl.ds(fields * STEPS, rest), :] = jnp.zeros(
                    (rest, lat), jnp.float32
                )
    pert_copy = [
        lon_copy(pert_edge.at[0], pert_halo.at[1], 2, 0),
        lon_copy(pert_edge.at[1], pert_halo.at[0], 2, 1),
    ]
    for copy in pert_copy:
        copy.start()

    lane = lax.broadcasted_iota(jnp.int32, (rows, lat), 1)
    not_north = jnp.where(lane == lat - 1, 0.0, 1.0)
    not_south = jnp.where(lane == 0, 0.0, 1.0)

    def from_west(q):
        return pltpu.roll(q, 1, 0)

    def from_east(q):
        return pltpu.roll(q, rows - 1, 0)

    def from_south(q):
        return pltpu.roll(q, 1, 1)

    def from_north(q):
        return pltpu.roll(q, lat - 1, 1)

    def faces(level, _):
        k = kap[level]
        to_east = (0.5 * TIME_STEP) * (k + from_east(k))
        to_north = (0.5 * TIME_STEP) * (k + from_north(k)) * not_north
        face[0, level] = to_east
        face[1, level] = from_west(to_east)
        face[2, level] = to_north
        face[3, level] = from_south(to_north)
        return 0

    def coefficients(u, v, level):
        u = TIME_STEP * u
        v = TIME_STEP * v
        to_e = face[0, level] - jnp.minimum(u, 0.0)
        to_w = face[1, level] + jnp.maximum(u, 0.0)
        to_n = face[2, level] - jnp.minimum(v, 0.0) * not_north
        to_s = face[3, level] + jnp.maximum(v, 0.0) * not_south
        here = 1.0 - ((to_e + to_w) + (to_n + to_s))
        return to_e, to_w, to_n, to_s, here

    def moved(q, c):
        to_e, to_w, to_n, to_s, here = c
        return (
            here * q
            + (to_e * from_east(q) + to_w * from_west(q))
            + (to_n * from_north(q) + to_s * from_south(q))
        )

    def observed(t):
        inner = t[EDGE : EDGE + width, :]
        terms = weight[...] * inner * inner
        return jnp.sum(terms.reshape(width // 8, 8, lat), axis=0)

    def own_level(level, total):
        u, v, t = own[0, level], own[1, level], own[2, level]
        for step in range(STEPS):
            c = coefficients(u, v, level)
            t_next = moved(t, c)
            if step < STEPS - 1:
                u, v = moved(u, c), moved(v, c)
            t = t_next
            total = total + observed(t)
        return total

    def share(which):
        return [
            pltpu.make_async_remote_copy(
                src_ref=part.at[which, lon],
                dst_ref=part.at[which, lon],
                send_sem=s_send.at[which, d - 1],
                recv_sem=s_recv.at[which, d - 1],
                device_id={"lon": lax.rem(lon + d, ring)},
                device_id_type=MESH_ID,
            )
            for d in range(1, ring)
        ]

    def arrive(kind, level):
        for k in range(1, groups):
            across(k, kind, level).wait_recv()
            to_twin(k, kind, level).start()

    def settled(kind, level):
        for k in range(groups):
            to_twin(k, kind, level).wait_recv()

    arrive("lo", 0)
    arrive("hi", 0)
    settled("lo", 0)
    settled("hi", 0)
    ancestor = anc_ref[0]

    def pick(load):
        value = load(0)
        for j in range(1, n):
            value = jnp.where(ancestor == j, load(j), value)
        return value

    def pick_edges(f):
        for level in range(levels):
            lower = pick(lambda j: full[j, f, level, 0:EDGE, :])
            upper = pick(lambda j: full[j, f, level, top:width, :])
            edge[0, f, level] = lower
            edge[1, f, level] = upper
            state[f, level, EDGE : 2 * EDGE, :] = lower
            state[f, level, width : width + EDGE, :] = upper

    def pass_edges(fs, slot):
        return [
            lon_copy(edge.at[0, fs], state.at[fs, :, high], slot, 0),
            lon_copy(edge.at[1, fs], state.at[fs, :, low], slot, 1),
        ]

    for f in range(dyn):
        pick_edges(f)
    edge_copy = pass_edges(pl.ds(0, dyn), 3)
    for copy in edge_copy:
        copy.start()
    arrive("hum_lo", 0)
    arrive("hum_hi", 0)
    settled("hum_lo", 0)
    settled("hum_hi", 0)
    pick_edges(dyn)
    hum_edge_copy = pass_edges(dyn, 4)
    for copy in hum_edge_copy + own_halo:
        copy.start()
    for copy in kap_halo:
        copy.wait()
    lax.fori_loop(0, levels, faces, 0)
    first_share = share(0)

    for level in range(levels - 2):
        arrive("dyn", level)
    for copy in pert_copy + edge_copy:
        copy.wait()

    def fill(f, level):
        state[f, level, 2 * EDGE : width, :] = pick(
            lambda j: full[j, f, level, EDGE : width - EDGE, :]
        )
        return state[f, level]

    def noise(f, level):
        spot = slice(f * STEPS, (f + 1) * STEPS)
        blank = jnp.zeros((EDGE - STEPS, lat), jnp.float32)
        lower, upper = pert_halo[0, level, spot, :], pert_halo[1, level, spot, :]
        return jnp.concatenate([blank, lower, pert[chosen, f, level], upper, blank], axis=0)

    def dyn_level(level, total):
        settled("dyn", level)
        u, v, t = fill(0, level), fill(1, level), fill(2, level)
        for step in range(2 * STEPS):
            if step == STEPS:
                u, v, t = u + noise(0, level), v + noise(1, level), t + noise(2, level)
            c = coefficients(u, v, level)
            for i in range(5):
                coef[level, step, i] = c[i]
            u, v, t = moved(u, c), moved(v, c), moved(t, c)
            if step >= STEPS:
                total = total + observed(t)
        inner = slice(EDGE, EDGE + width)
        out_ref[0, 0, level] = u[inner]
        out_ref[0, 1, level] = v[inner]
        out_ref[0, 2, level] = t[inner]

        @pl.when(level == 0)
        def _():
            arrive("dyn", levels - 2)

        @pl.when(level == levels - 2)
        def _():
            arrive("dyn", levels - 1)
            for copy in own_halo:
                copy.wait()
            part[0, lon] = lax.fori_loop(
                0, levels, own_level, jnp.zeros((8, lat), jnp.float32)
            )
            for copy in first_share:
                copy.start()
            arrive("hum", 0)

        return total

    part[1, lon] = lax.fori_loop(0, levels, dyn_level, jnp.zeros((8, lat), jnp.float32))
    second_share = share(1)
    for copy in second_share:
        copy.start()

    arrive("hum", 1)
    for copy in hum_edge_copy:
        copy.wait()

    def hum_level(level, carry):
        @pl.when(level < levels - 2)
        def _():
            arrive("hum", level + 2)

        settled("hum", level)
        q = fill(dyn, level)
        for step in range(2 * STEPS):
            if step == STEPS:
                q = q + noise(dyn, level)
            q = moved(q, [coef[level, step, i] for i in range(5)])
        out_ref[0, dyn, level] = q[EDGE : EDGE + width]
        return carry

    lax.fori_loop(0, levels, hum_level, 0)

    cells = levels * lat * width * ring
    action = []
    for which, copies in enumerate((first_share, second_share)):
        for copy in copies:
            copy.wait()
        action.append(jnp.sum(jnp.sum(part[which], axis=0)) / cells)
    column = lax.broadcasted_iota(jnp.int32, (1, 2), 1)
    act_ref[...] = jnp.where(column == 0, action[0], action[1])
    for kind, level in pieces:
        for k in range(1, groups):
            across(k, kind, level).wait_send()
        for k in range(groups):
            to_twin(k, kind, level).wait_send()


def body(initial_state, ancestor, selector, perturbations, diffusivity, region_weight):
    n, ring = lax.axis_size("mem"), lax.axis_size("lon")
    _, fields, levels, width, lat = initial_state.shape
    rows = width + 2 * EDGE
    kinds = 4 + 2 * levels
    packed = -(-fields * STEPS // 8) * 8
    f32 = jnp.float32
    any_space = pl.BlockSpec(memory_space=pltpu.HBM)
    dma = pltpu.SemaphoreType.DMA
    return pl.pallas_call(
        functools.partial(kernel, n, ring),
        out_shape=(
            pltpu.VMEM(initial_state.shape, f32),
            pltpu.VMEM((1, 2), f32),
        ),
        in_specs=[any_space] * 6,
        out_specs=(pl.BlockSpec(memory_space=pltpu.VMEM),) * 2,
        scratch_shapes=[
            pltpu.VMEM((n, fields, levels, width, lat), f32),
            pltpu.VMEM((fields, levels, rows, lat), f32),
            pltpu.VMEM((fields - 1, levels, rows, lat), f32),
            pltpu.VMEM(perturbations.shape, f32),
            pltpu.VMEM((2, levels, packed, lat), f32),
            pltpu.VMEM((2, levels, packed, lat), f32),
            pltpu.VMEM((2, fields, levels, EDGE, lat), f32),
            pltpu.VMEM((levels, rows, lat), f32),
            pltpu.VMEM((4, levels, rows, lat), f32),
            pltpu.VMEM((levels, 2 * STEPS, 5, rows, lat), f32),
            pltpu.VMEM((width, lat), f32),
            pltpu.VMEM((2, ring, 8, lat), f32),
            dma((n // 2 - 1, kinds)),
            dma((n // 2 - 1, kinds)),
            dma((n // 2, kinds)),
            dma((n // 2, kinds)),
            dma((5, 2)),
            dma((5, 2)),
            dma((2, ring - 1)),
            dma((2, ring - 1)),
            dma((7,)),
            pltpu.SemaphoreType.REGULAR((2,)),
            pltpu.SMEM((1,), jnp.int32),
            pltpu.SMEM((1,), jnp.int32),
        ],
        compiler_params=pltpu.CompilerParams(
            collective_id=0, has_side_effects=True, vmem_limit_bytes=VMEM_LIMIT
        ),
    )(ancestor, selector, initial_state, perturbations, diffusivity, region_weight)


def solution(mesh):
    in_specs = (
        P(("ens", "mem"), None, None, "lon", None),
        P(("ens", "mem")),
        P(("ens", "mem")),
        P("ens", None, None, "lon", None),
        P(None, "lon", None),
        P("lon", None),
    )
    out_specs = (P(("ens", "mem"), None, None, "lon", None), P(("ens", "mem"), None))
    return jax.shard_map(body, mesh=mesh, in_specs=in_specs, out_specs=out_specs, check_vma=False)
```

```python
import functools

import jax
import jax.numpy as jnp
from jax import lax
from jax.experimental import pallas as pl
from jax.experimental.pallas import tpu as pltpu
from jax.sharding import PartitionSpec as P

STEPS = 3
TIME_STEP = 0.2
EDGE = 8
VMEM_LIMIT = 66000000
MESH_ID = pl.DeviceIdType.MESH


def kernel(
    n, ring, anc_hbm, sel_hbm, init_ref, pert_ref, kap_ref, weight_ref, out_ref, act_ref,
    full, state, own, pert, pert_edge, pert_halo, edge, kap, face, coef, weight, part,
    x_send, x_recv, p_send, p_recv, z_send, z_recv, s_send, s_recv, local_sem,
    token, anc_ref, sel_ref,
):
    _, fields, levels, width, lat = init_ref.shape
    rows = width + 2 * EDGE
    dyn = fields - 1
    groups = n // 2
    mem = lax.axis_index("mem")
    lon = lax.axis_index("lon")
    twin = mem + 1 - 2 * lax.rem(mem, 2)
    east, west = lax.rem(lon + 1, ring), lax.rem(lon + ring - 1, ring)
    top = width - EDGE

    local = [
        pltpu.make_async_copy(init_ref.at[0], full.at[mem], local_sem.at[0]),
        pltpu.make_async_copy(
            init_ref.at[0, pl.ds(0, dyn)], own.at[:, :, pl.ds(EDGE, width)], local_sem.at[1]
        ),
        pltpu.make_async_copy(kap_ref, kap.at[:, pl.ds(EDGE, width)], local_sem.at[2]),
        pltpu.make_async_copy(weight_ref, weight, local_sem.at[3]),
        pltpu.make_async_copy(pert_ref, pert, local_sem.at[4]),
        pltpu.make_async_copy(anc_hbm, anc_ref, local_sem.at[5]),
        pltpu.make_async_copy(sel_hbm, sel_ref, local_sem.at[6]),
    ]
    for copy in local:
        copy.start()

    barrier = pltpu.get_barrier_semaphore()
    for k in range(1, groups):
        pl.semaphore_signal(
            barrier, inc=1, device_id={"mem": lax.rem(mem + 2 * k, n)}, device_id_type=MESH_ID
        )
    pl.semaphore_signal(barrier, inc=1, device_id={"mem": twin}, device_id_type=MESH_ID)

    def toward(semaphore, up):
        @pl.when(lon < ring - 1 if up else lon > 0)
        def _():
            pl.semaphore_signal(
                semaphore, inc=1, device_id={"lon": east if up else west}, device_id_type=MESH_ID
            )

    toward(barrier, True)
    toward(barrier, False)
    beside = jnp.where(lon > 0, 1, 0) + jnp.where(lon < ring - 1, 1, 0)
    pl.semaphore_wait(barrier, groups + beside)

    def pass_token(up):
        @pl.when(lon > 0 if up else lon < ring - 1)
        def _():
            pl.semaphore_wait(token.at[int(up)], 1)

        toward(token.at[int(up)], up)

    def view(block, kind, level):
        if kind == "lo":
            return block.at[pl.ds(0, dyn), :, pl.ds(0, EDGE)]
        if kind == "hi":
            return block.at[pl.ds(0, dyn), :, pl.ds(top, EDGE)]
        if kind == "hum_lo":
            return block.at[dyn, :, pl.ds(0, EDGE)]
        if kind == "hum_hi":
            return block.at[dyn, :, pl.ds(top, EDGE)]
        if kind == "dyn":
            return block.at[pl.ds(0, dyn), level, pl.ds(EDGE, width - 2 * EDGE)]
        return block.at[dyn, level, pl.ds(EDGE, width - 2 * EDGE)]

    def sem_of(kind, level):
        base = {"lo": 0, "hi": 1, "hum_lo": 2, "hum_hi": 3, "dyn": 4, "hum": 4 + levels}
        return base[kind] + level

    def across(k, kind, level):
        slot = sem_of(kind, level)
        return pltpu.make_async_remote_copy(
            src_ref=view(init_ref.at[0], kind, level),
            dst_ref=view(full.at[mem], kind, level),
            send_sem=x_send.at[k - 1, slot],
            recv_sem=x_recv.at[k - 1, slot],
            device_id={"mem": lax.rem(mem + 2 * k, n)},
            device_id_type=MESH_ID,
        )

    def to_twin(k, kind, level):
        slot = sem_of(kind, level)
        member = lax.rem(mem + n - 2 * k, n)
        source = init_ref.at[0] if k == 0 else full.at[member]
        return pltpu.make_async_remote_copy(
            src_ref=view(source, kind, level),
            dst_ref=view(full.at[member], kind, level),
            send_sem=p_send.at[k, slot],
            recv_sem=p_recv.at[k, slot],
            device_id={"mem": twin},
            device_id_type=MESH_ID,
        )

    def lon_copy(source, target, slot, side):
        return pltpu.make_async_remote_copy(
            src_ref=source,
            dst_ref=target,
            send_sem=z_send.at[slot, side],
            recv_sem=z_recv.at[slot, side],
            device_id={"lon": east if side else west},
            device_id_type=MESH_ID,
        )

    low, high = pl.ds(0, EDGE), pl.ds(EDGE + width, EDGE)
    first, last = pl.ds(0, EDGE), pl.ds(top, EDGE)
    pieces = [("lo", 0), ("hi", 0), ("hum_lo", 0), ("hum_hi", 0)]
    pieces += [("dyn", level) for level in range(levels)]
    pieces += [("hum", level) for level in range(levels)]
    for kind, level in pieces:
        for k in range(1, groups):
            across(k, kind, level).start()
    own_halo = [
        lon_copy(init_ref.at[0, pl.ds(0, dyn), :, first], own.at[:, :, high], 0, 0),
        lon_copy(init_ref.at[0, pl.ds(0, dyn), :, last], own.at[:, :, low], 0, 1),
    ]
    kap_halo = [
        lon_copy(kap_ref.at[:, first], kap.at[:, high], 1, 0),
        lon_copy(kap_ref.at[:, last], kap.at[:, low], 1, 1),
    ]

    def start_halo(near):
        for side, inside in enumerate((lon > 0, lon < ring - 1)):

            @pl.when(inside if near else jnp.logical_not(inside))
            def _():
                kap_halo[side].start()
                own_halo[side].start()

    start_halo(True)
    for kind, level in pieces:
        to_twin(0, kind, level).start()

    @pl.when(2 * lon < ring)
    def _():
        pass_token(True)
        pass_token(False)

    @pl.when(2 * lon >= ring)
    def _():
        pass_token(False)
        pass_token(True)

    start_halo(False)

    for copy in local:
        copy.wait()
    chosen = sel_ref[0]
    packed = pert_edge.shape[2]
    for level in range(levels):
        for f in range(fields):
            spot = pl.ds(f * STEPS, STEPS)
            pert_edge[0, level, spot, :] = pert[chosen, f, level, 0:STEPS, :]
            pert_edge[1, level, spot, :] = pert[chosen, f, level, width - STEPS : width, :]
        if packed > fields * STEPS:
            rest = packed - fields * STEPS
            for side in range(2):
                pert_edge[side, level, pl.ds(fields * STEPS, rest), :] = jnp.zeros(
                    (rest, lat), jnp.float32
                )
    pert_copy = [
        lon_copy(pert_edge.at[0], pert_halo.at[1], 2, 0),
        lon_copy(pert_edge.at[1], pert_halo.at[0], 2, 1),
    ]
    for copy in pert_copy:
        copy.start()

    lane = lax.broadcasted_iota(jnp.int32, (rows, lat), 1)
    not_north = jnp.where(lane == lat - 1, 0.0, 1.0)
    not_south = jnp.where(lane == 0, 0.0, 1.0)

    def from_west(q):
        return pltpu.roll(q, 1, 0)

    def from_east(q):
        return pltpu.roll(q, rows - 1, 0)

    def from_south(q):
        return pltpu.roll(q, 1, 1)

    def from_north(q):
        return pltpu.roll(q, lat - 1, 1)

    def faces(level, _):
        k = kap[level]
        to_east = (0.5 * TIME_STEP) * (k + from_east(k))
        to_north = (0.5 * TIME_STEP) * (k + from_north(k)) * not_north
        face[0, level] = to_east
        face[1, level] = from_west(to_east)
        face[2, level] = to_north
        face[3, level] = from_south(to_north)
        return 0

    def coefficients(u, v, level):
        u = TIME_STEP * u
        v = TIME_STEP * v
        to_e = face[0, level] - jnp.minimum(u, 0.0)
        to_w = face[1, level] + jnp.maximum(u, 0.0)
        to_n = face[2, level] - jnp.minimum(v, 0.0) * not_north
        to_s = face[3, level] + jnp.maximum(v, 0.0) * not_south
        here = 1.0 - ((to_e + to_w) + (to_n + to_s))
        return to_e, to_w, to_n, to_s, here

    def moved(q, c):
        to_e, to_w, to_n, to_s, here = c
        return (
            here * q
            + (to_e * from_east(q) + to_w * from_west(q))
            + (to_n * from_north(q) + to_s * from_south(q))
        )

    def observed(t):
        inner = t[EDGE : EDGE + width, :]
        terms = weight[...] * inner * inner
        return jnp.sum(terms.reshape(width // 8, 8, lat), axis=0)

    def own_level(level, total):
        u, v, t = own[0, level], own[1, level], own[2, level]
        for step in range(STEPS):
            c = coefficients(u, v, level)
            t_next = moved(t, c)
            if step < STEPS - 1:
                u, v = moved(u, c), moved(v, c)
            t = t_next
            total = total + observed(t)
        return total

    def share(which):
        return [
            pltpu.make_async_remote_copy(
                src_ref=part.at[which, lon],
                dst_ref=part.at[which, lon],
                send_sem=s_send.at[which, d - 1],
                recv_sem=s_recv.at[which, d - 1],
                device_id={"lon": lax.rem(lon + d, ring)},
                device_id_type=MESH_ID,
            )
            for d in range(1, ring)
        ]

    def arrive(kind, level):
        for k in range(1, groups):
            across(k, kind, level).wait_recv()
            to_twin(k, kind, level).start()

    def settled(kind, level):
        for k in range(groups):
            to_twin(k, kind, level).wait_recv()

    arrive("lo", 0)
    arrive("hi", 0)
    settled("lo", 0)
    settled("hi", 0)
    ancestor = anc_ref[0]

    def pick(load):
        value = load(0)
        for j in range(1, n):
            value = jnp.where(ancestor == j, load(j), value)
        return value

    def pick_edges(f):
        for level in range(levels):
            lower = pick(lambda j: full[j, f, level, 0:EDGE, :])
            upper = pick(lambda j: full[j, f, level, top:width, :])
            edge[0, f, level] = lower
            edge[1, f, level] = upper
            state[f, level, EDGE : 2 * EDGE, :] = lower
            state[f, level, width : width + EDGE, :] = upper

    def pass_edges(fs, slot):
        return [
            lon_copy(edge.at[0, fs], state.at[fs, :, high], slot, 0),
            lon_copy(edge.at[1, fs], state.at[fs, :, low], slot, 1),
        ]

    for f in range(dyn):
        pick_edges(f)
    edge_copy = pass_edges(pl.ds(0, dyn), 3)
    for copy in edge_copy:
        copy.start()
    arrive("hum_lo", 0)
    arrive("hum_hi", 0)
    settled("hum_lo", 0)
    settled("hum_hi", 0)
    pick_edges(dyn)
    hum_edge_copy = pass_edges(dyn, 4)
    for copy in hum_edge_copy:
        copy.start()

    for copy in kap_halo + own_halo:
        copy.wait()
    lax.fori_loop(0, levels, faces, 0)
    part[0, lon] = lax.fori_loop(0, levels, own_level, jnp.zeros((8, lat), jnp.float32))
    first_share = share(0)
    for copy in first_share:
        copy.start()

    for level in range(levels - 2):
        arrive("dyn", level)
    for copy in pert_copy + edge_copy:
        copy.wait()

    def fill(f, level):
        state[f, level, 2 * EDGE : width, :] = pick(
            lambda j: full[j, f, level, EDGE : width - EDGE, :]
        )
        return state[f, level]

    def noise(f, level):
        spot = slice(f * STEPS, (f + 1) * STEPS)
        blank = jnp.zeros((EDGE - STEPS, lat), jnp.float32)
        lower, upper = pert_halo[0, level, spot, :], pert_halo[1, level, spot, :]
        return jnp.concatenate([blank, lower, pert[chosen, f, level], upper, blank], axis=0)

    def dyn_level(level, total):
        settled("dyn", level)
        u, v, t = fill(0, level), fill(1, level), fill(2, level)
        for step in range(2 * STEPS):
            if step == STEPS:
                u, v, t = u + noise(0, level), v + noise(1, level), t + noise(2, level)
            c = coefficients(u, v, level)
            for i in range(5):
                coef[level, step, i] = c[i]
            u, v, t = moved(u, c), moved(v, c), moved(t, c)
            if step >= STEPS:
                total = total + observed(t)
        inner = slice(EDGE, EDGE + width)
        out_ref[0, 0, level] = u[inner]
        out_ref[0, 1, level] = v[inner]
        out_ref[0, 2, level] = t[inner]

        @pl.when(level == 0)
        def _():
            arrive("dyn", levels - 2)

        @pl.when(level == levels - 2)
        def _():
            arrive("dyn", levels - 1)
            arrive("hum", 0)

        return total

    part[1, lon] = lax.fori_loop(0, levels, dyn_level, jnp.zeros((8, lat), jnp.float32))
    second_share = share(1)
    for copy in second_share:
        copy.start()

    arrive("hum", 1)
    for copy in hum_edge_copy:
        copy.wait()

    def hum_level(level, carry):
        @pl.when(level < levels - 2)
        def _():
            arrive("hum", level + 2)

        settled("hum", level)
        q = fill(dyn, level)
        for step in range(2 * STEPS):
            if step == STEPS:
                q = q + noise(dyn, level)
            q = moved(q, [coef[level, step, i] for i in range(5)])
        out_ref[0, dyn, level] = q[EDGE : EDGE + width]
        return carry

    lax.fori_loop(0, levels, hum_level, 0)

    cells = levels * lat * width * ring
    action = []
    for which, copies in enumerate((first_share, second_share)):
        for copy in copies:
            copy.wait()
        action.append(jnp.sum(jnp.sum(part[which], axis=0)) / cells)
    column = lax.broadcasted_iota(jnp.int32, (1, 2), 1)
    act_ref[...] = jnp.where(column == 0, action[0], action[1])
    for kind, level in pieces:
        for k in range(1, groups):
            across(k, kind, level).wait_send()
        for k in range(groups):
            to_twin(k, kind, level).wait_send()


def body(initial_state, ancestor, selector, perturbations, diffusivity, region_weight):
    n, ring = lax.axis_size("mem"), lax.axis_size("lon")
    _, fields, levels, width, lat = initial_state.shape
    rows = width + 2 * EDGE
    kinds = 4 + 2 * levels
    packed = -(-fields * STEPS // 8) * 8
    f32 = jnp.float32
    any_space = pl.BlockSpec(memory_space=pltpu.HBM)
    dma = pltpu.SemaphoreType.DMA
    return pl.pallas_call(
        functools.partial(kernel, n, ring),
        out_shape=(
            pltpu.VMEM(initial_state.shape, f32),
            pltpu.VMEM((1, 2), f32),
        ),
        in_specs=[any_space] * 6,
        out_specs=(pl.BlockSpec(memory_space=pltpu.VMEM),) * 2,
        scratch_shapes=[
            pltpu.VMEM((n, fields, levels, width, lat), f32),
            pltpu.VMEM((fields, levels, rows, lat), f32),
            pltpu.VMEM((fields - 1, levels, rows, lat), f32),
            pltpu.VMEM(perturbations.shape, f32),
            pltpu.VMEM((2, levels, packed, lat), f32),
            pltpu.VMEM((2, levels, packed, lat), f32),
            pltpu.VMEM((2, fields, levels, EDGE, lat), f32),
            pltpu.VMEM((levels, rows, lat), f32),
            pltpu.VMEM((4, levels, rows, lat), f32),
            pltpu.VMEM((levels, 2 * STEPS, 5, rows, lat), f32),
            pltpu.VMEM((width, lat), f32),
            pltpu.VMEM((2, ring, 8, lat), f32),
            dma((n // 2 - 1, kinds)),
            dma((n // 2 - 1, kinds)),
            dma((n // 2, kinds)),
            dma((n // 2, kinds)),
            dma((5, 2)),
            dma((5, 2)),
            dma((2, ring - 1)),
            dma((2, ring - 1)),
            dma((7,)),
            pltpu.SemaphoreType.REGULAR((2,)),
            pltpu.SMEM((1,), jnp.int32),
            pltpu.SMEM((1,), jnp.int32),
        ],
        compiler_params=pltpu.CompilerParams(
            collective_id=0, has_side_effects=True, vmem_limit_bytes=VMEM_LIMIT
        ),
    )(ancestor, selector, initial_state, perturbations, diffusivity, region_weight)


def solution(mesh):
    in_specs = (
        P(("ens", "mem"), None, None, "lon", None),
        P(("ens", "mem")),
        P(("ens", "mem")),
        P("ens", None, None, "lon", None),
        P(None, "lon", None),
        P("lon", None),
    )
    out_specs = (P(("ens", "mem"), None, None, "lon", None), P(("ens", "mem"), None))
    return jax.shard_map(body, mesh=mesh, in_specs=in_specs, out_specs=out_specs, check_vma=False)
```
